32 devices in a mesh: fsdp: 4 (over z), ctx: 4 (over y, x), tp: 2 (over core).
Axes of the slice: x: 2, y: 2, z: 4, core: 2. Of those that a mesh axis runs over, the one named last changes fastest.
Arguments:
- inputs: bfloat16 [8, 512, 768], P('fsdp', 'ctx'), may hold values from -6 to 6
- cotangent: bfloat16 [8, 512, 768], P('fsdp', 'ctx'), may hold values from -6 to 6
- seq_lengths: int32 [8], replicated, may hold values from 128 to 384, as said below
- seq_slots: int32 [8], replicated, may hold values from 0 to 7, as said below
- offsets: int32 [8], replicated, may hold values from 0 to 384, as said below
- query_weight: bfloat16 [768, 768], P(('fsdp', 'ctx'), 'tp'), may hold values from -0.21875 to 0.21875
- key_weight: bfloat16 [768, 768], P(('fsdp', 'ctx'), 'tp'), may hold values from -0.21875 to 0.21875
- value_weight: bfloat16 [768, 768], P(('fsdp', 'ctx'), 'tp'), may hold values from -0.21875 to 0.21875
- query_bias: bfloat16 [2, 384], P('tp', ('fsdp', 'ctx')), may hold values from -4 to 4
- value_bias: bfloat16 [2, 384], P('tp', ('fsdp', 'ctx')), may hold values from -4 to 4
- out_weight: bfloat16 [768, 768], P('tp', ('fsdp', 'ctx')), may hold values from -1.25 to 1.25
- out_bias: bfloat16 [768], P(('fsdp', 'ctx')), may hold values from -4 to 4
- attn_gain: bfloat16 [768], P(('fsdp', 'ctx')), may hold values from 0.5 to 1.5
- attn_shift: bfloat16 [768], P(('fsdp', 'ctx')), may hold values from -4 to 4
- up_weight: bfloat16 [768, 3072], P(('fsdp', 'ctx'), 'tp'), may hold values from -0.21875 to 0.21875
- up_bias: bfloat16 [2, 1536], P('tp', ('fsdp', 'ctx')), may hold values from -4 to 4
- down_weight: bfloat16 [3072, 768], P('tp', ('fsdp', 'ctx')), may hold values from -0.109375 to 0.109375
- down_bias: bfloat16 [768], P(('fsdp', 'ctx')), may hold values from -4 to 4
- ffn_gain: bfloat16 [768], P(('fsdp', 'ctx')), may hold values from 0.5 to 1.5
- ffn_shift: bfloat16 [768], P(('fsdp', 'ctx')), may hold values from -4 to 4
Outputs:
- outputs: bfloat16 [8, 512, 768], P('fsdp', 'ctx')
- input_grad: bfloat16 [8, 512, 768], P('fsdp', 'ctx')
- query_weight_grad: float32 [768, 768], P(('fsdp', 'ctx'), 'tp')
- key_weight_grad: float32 [768, 768], P(('fsdp', 'ctx'), 'tp')
- value_weight_grad: float32 [768, 768], P(('fsdp', 'ctx'), 'tp')
- query_bias_grad: float32 [2, 384], P('tp', ('fsdp', 'ctx'))
- value_bias_grad: float32 [2, 384], P('tp', ('fsdp', 'ctx'))
- out_weight_grad: float32 [768, 768], P('tp', ('fsdp', 'ctx'))
- out_bias_grad: float32 [768], P(('fsdp', 'ctx'))
- attn_gain_grad: float32 [768], P(('fsdp', 'ctx'))
- attn_shift_grad: float32 [768], P(('fsdp', 'ctx'))
- up_weight_grad: float32 [768, 3072], P(('fsdp', 'ctx'), 'tp')
- up_bias_grad: float32 [2, 1536], P('tp', ('fsdp', 'ctx'))
- down_weight_grad: float32 [3072, 768], P('tp', ('fsdp', 'ctx'))
- down_bias_grad: float32 [768], P(('fsdp', 'ctx'))
- ffn_gain_grad: float32 [768], P(('fsdp', 'ctx'))
- ffn_shift_grad: float32 [768], P(('fsdp', 'ctx'))
The draws below stay inside these ranges and needn't reach their ends.
Inputs may be any that keep to these rules, and one draw needn't show every extreme that they name: `seq_lengths`: the two sequences dealt to one group together hold at most 512 tokens, exactly 512 in some group. A permutation of 0 to 7: sequence s is number seq_slots[s] % 2 of group seq_slots[s] // 2. `offsets`: 0 for the first sequence of a group; for the second, the first one's length.
All inputs are finite; a program needn't handle non-finite values.
Results may differ from the reference program's by a relative error of at most 0.019.
Values may be sent and summed in bfloat16 or wider, within the bound.
No kernel may reach another device: no remote copies, remote signals or barrier semaphores. Data moves between devices by JAX's collectives and lax.ppermute only.
A program may use at most 128 MiB of HBM per device.

```python
import jax
import jax.numpy as jnp
from jax import lax

D = 768
HEADS = 12
HD = 64
FF = 3072
MIN_LEN = 1024
CAP = 512
GROUPS = 4
NSEQ = 8


def dealt_sequences(key):
    first_key, second_key, pick_key, order_key = jax.random.split(jax.random.fold_in(key, 11), 4)
    lowest = min(MIN_LEN, CAP // 4)
    group_numbers = jnp.arange(GROUPS, dtype=jnp.int32)
    first_len = jax.random.randint(first_key, (GROUPS,), lowest, CAP - lowest + 1)
    full_group = jax.random.randint(pick_key, (), 0, GROUPS)
    long_group = (full_group + 1) % GROUPS
    first_len = jnp.where(group_numbers == long_group, CAP - lowest, first_len)
    room_left = CAP - first_len
    second_len = jax.random.randint(second_key, (GROUPS,), lowest, room_left + 1)
    second_len = jnp.where((group_numbers == full_group) | (group_numbers == long_group), room_left, second_len)
    slot_lengths = jnp.stack([first_len, second_len], axis=1).reshape(NSEQ).astype(jnp.int32)
    slot_offsets = jnp.stack([jnp.zeros_like(first_len), first_len], axis=1).reshape(NSEQ).astype(jnp.int32)
    seq_slots = jax.random.permutation(order_key, NSEQ).astype(jnp.int32)
    return (slot_lengths[seq_slots], seq_slots, slot_offsets[seq_slots])


def draw_seq_lengths(key, part):
    return dealt_sequences(key)[0]


def draw_seq_slots(key, part):
    return dealt_sequences(key)[1]


def draw_offsets(key, part):
    return dealt_sequences(key)[2]


def shard_levels(rng, extent, cuts, low, top_value):
    factor_of, own = 1.0, jax.random.fold_in(rng, 6)
    for position, shards_of in cuts:
        draws = jnp.exp(jax.random.uniform(jax.random.fold_in(own, position), (shards_of,), jnp.float32, low / len(cuts), top_value / len(cuts)))
        factor_of = factor_of * jnp.repeat(draws, extent[position] // shards_of).reshape([-1 if axis == position else 1 for axis in range(len(extent))])
    return factor_of


def bell_draw(stream_key, dims, scale, most, shards=(), kind=jnp.bfloat16):
    loudness = shard_levels(stream_key, dims, shards, -0.22, 0.18) if shards else 1.0
    array = jax.random.normal(stream_key, dims, jnp.float32) * scale * loudness
    return jnp.minimum(jnp.maximum(array, -most), most).astype(kind)


def setup_inputs(seed: int = 0) -> dict:
    streams_of = jax.random.split(jax.random.key(seed), 21)
    return {
        "inputs": bell_draw(streams_of[0], (NSEQ, CAP, D), 1.0, 6.0, ((0, 4), (1, 4))),
        "cotangent": bell_draw(streams_of[1], (NSEQ, CAP, D), 1.0, 6.0, ((0, 4), (1, 4))),
        "seq_lengths": draw_seq_lengths(jax.random.fold_in(streams_of[20], 71), 0),
        "seq_slots": draw_seq_slots(jax.random.fold_in(streams_of[20], 71), 0),
        "offsets": draw_offsets(jax.random.fold_in(streams_of[20], 71), 0),
        "query_weight": bell_draw(streams_of[5], (D, D), D ** -0.5, 0.21875, ((0, 16), (1, 2))),
        "key_weight": bell_draw(streams_of[6], (D, D), D ** -0.5, 0.21875, ((0, 16), (1, 2))),
        "value_weight": bell_draw(streams_of[7], (D, D), D ** -0.5, 0.21875, ((0, 16), (1, 2))),
        "query_bias": bell_draw(streams_of[8], (2, D // 2), 0.3, 4.0, ((0, 2), (1, 16))),
        "value_bias": bell_draw(streams_of[9], (2, D // 2), 0.3, 4.0, ((0, 2), (1, 16))),
        "out_weight": bell_draw(streams_of[10], (D, D), (max(1, D * 16 // CAP)) ** -0.5, 1.25, ((0, 2), (1, 16))),
        "out_bias": bell_draw(streams_of[11], (D,), 0.3, 4.0, ((0, 16),)),
        "attn_gain": jnp.clip(1.0 + 0.1 * jax.random.normal(streams_of[12], (D,), jnp.float32), 0.5, 1.5).astype(jnp.bfloat16),
        "attn_shift": bell_draw(streams_of[13], (D,), 0.3, 4.0, ((0, 16),)),
        "up_weight": bell_draw(streams_of[14], (D, FF), D ** -0.5, 0.21875, ((0, 16), (1, 2))),
        "up_bias": bell_draw(streams_of[15], (2, FF // 2), 0.3, 4.0, ((0, 2), (1, 16))),
        "down_weight": bell_draw(streams_of[16], (FF, D), FF ** -0.5, 0.109375, ((0, 2), (1, 16))),
        "down_bias": bell_draw(streams_of[17], (D,), 0.3, 4.0, ((0, 16),)),
        "ffn_gain": jnp.clip(1.0 + 0.1 * jax.random.normal(streams_of[18], (D,), jnp.float32), 0.5, 1.5).astype(jnp.bfloat16),
        "ffn_shift": bell_draw(streams_of[19], (D,), 0.3, 4.0, ((0, 16),)),
    }


@jax.custom_vjp
def low(v):
    return lax.optimization_barrier(v.astype(jnp.bfloat16)).astype(jnp.float32)

@jax.custom_vjp
def low_back(v):
    return v

def low_keep(v):
    return (low(v), None)

def low_pass(kept, grad):
    return (grad,)

def back_keep(v):
    return (v, None)

def back_low(kept, grad):
    return (low(grad),)
low.defvjp(low_keep, low_pass)
low_back.defvjp(back_keep, back_low)
norm_epsilon = 1e-12
masked_score = -1000000000.0
highest = lax.Precision.HIGHEST

def matmul_high(left_side, right_side):
    return jnp.dot(left_side, right_side, precision=highest)

def layer_norm(values, norm_gain, norm_shift):
    centre = lax.optimization_barrier(jnp.mean(values, axis=-1, keepdims=True))
    centred = values - centre
    variance = lax.optimization_barrier(jnp.mean(centred * centred, axis=-1, keepdims=True))
    return centred * lax.rsqrt(variance + norm_epsilon) * norm_gain + norm_shift

def group_segments(group_index, seq_lengths, seq_slots, offsets, capacity):
    positions = jnp.arange(capacity, dtype=jnp.int32)
    member = (seq_slots // 2 == group_index)[:, None] & (offsets[:, None] <= positions[None, :]) & (positions[None, :] < (offsets + seq_lengths)[:, None])
    numbers = jnp.arange(seq_lengths.shape[0], dtype=jnp.int32) + 1
    return lax.optimization_barrier(jnp.sum(jnp.where(member, numbers[:, None], 0), axis=0)).astype(jnp.int32) - 1

def group_forward(inputs, params, segments):
    query_weight, key_weight, value_weight, query_bias, value_bias, out_weight, out_bias, attn_gain, attn_shift, up_weight, up_bias, down_weight, down_bias, ffn_gain, ffn_shift = params
    queries = low(low_back(matmul_high(inputs, query_weight) + query_bias.reshape(-1)))
    keys = low(low_back(matmul_high(inputs, key_weight)))
    values = low(low_back(matmul_high(inputs, value_weight) + value_bias.reshape(-1)))
    key_heads = keys.reshape(CAP, HEADS, HD)
    value_heads = values.reshape(CAP, HEADS, HD)
    positions = jnp.arange(CAP, dtype=jnp.int32)
    query_rows = min(CAP, 1024)
    block_count = CAP // query_rows

    def attend(block_data):
        block_queries, block_segments, block_positions = block_data
        raw_scores = low_back(jnp.einsum('qhd,khd->hqk', block_queries, key_heads, precision=highest))
        scores = raw_scores * HD ** (-0.5)
        allowed = (block_segments[:, None] == segments[None, :]) & (block_segments[:, None] >= 0) | (block_positions[:, None] == positions[None, :])
        scores = jnp.where(allowed[None], scores, masked_score)
        weights = low(jax.nn.softmax(scores, axis=-1))
        return low(low_back(jnp.einsum('hqk,khd->qhd', weights, value_heads, precision=highest)))
    attended = lax.map(jax.checkpoint(attend), (queries.reshape(block_count, query_rows, HEADS, HD), segments.reshape(block_count, query_rows), positions.reshape(block_count, query_rows)))
    context = attended.reshape(CAP, D)
    branch = low_back(matmul_high(context, out_weight) + out_bias)
    mixed = layer_norm(inputs + branch, attn_gain, attn_shift)
    pre_act = low_back(matmul_high(low(mixed), up_weight) + up_bias.reshape(-1))
    activated = low(jax.nn.gelu(pre_act, approximate=False))
    ffn_branch = low_back(matmul_high(activated, down_weight) + down_bias)
    return layer_norm(mixed + ffn_branch, ffn_gain, ffn_shift)

def reference(inputs, cotangent, seq_lengths, seq_slots, offsets, query_weight, key_weight, value_weight, query_bias, value_bias, out_weight, out_bias, attn_gain, attn_shift, up_weight, up_bias, down_weight, down_bias, ffn_gain, ffn_shift):
    params = tuple((weight_arg.astype(jnp.float32) for weight_arg in (query_weight, key_weight, value_weight, query_bias, value_bias, out_weight, out_bias, attn_gain, attn_shift, up_weight, up_bias, down_weight, down_bias, ffn_gain, ffn_shift)))
    wide_inputs = inputs.astype(jnp.float32)
    wide_cotangent = cotangent.astype(jnp.float32)
    zero_grads = tuple((jnp.zeros(weight_arg.shape, jnp.float32) for weight_arg in params))
    positions = jnp.arange(CAP, dtype=jnp.int32)

    def one_group(totals, group_index):
        segments = group_segments(group_index, seq_lengths, seq_slots, offsets, CAP)
        live = segments >= 0
        safe_seq = jnp.maximum(segments, 0).astype(jnp.int32)
        seq_pos = jnp.clip(positions - offsets[safe_seq], 0, CAP - 1).astype(jnp.int32)
        group_in = jnp.where(live[:, None], wide_inputs[safe_seq, seq_pos], jnp.zeros((), wide_inputs.dtype))
        group_cot = jnp.where(live[:, None], wide_cotangent[safe_seq, seq_pos], jnp.zeros((), wide_cotangent.dtype))

        def run_layer(values_in, weight_set):
            return group_forward(values_in, weight_set, segments)
        result, backward = jax.vjp(run_layer, group_in, params)
        input_part, param_parts = backward(group_cot)
        totals = tuple((summed + added for summed, added in zip(totals, param_parts)))
        return (totals, (result.astype(jnp.bfloat16), input_part.astype(jnp.bfloat16)))
    totals, (results, input_parts) = lax.scan(one_group, zero_grads, jnp.arange(GROUPS, dtype=jnp.int32))
    seq_group = (seq_slots // 2).astype(jnp.int32)
    packed_pos = jnp.clip(offsets[:, None] + positions[None, :], 0, CAP - 1).astype(jnp.int32)
    live_rows = positions[None, :] < seq_lengths[:, None]
    outputs = jnp.where(live_rows[..., None], results[seq_group[:, None], packed_pos], jnp.zeros((), jnp.bfloat16))
    input_grad = jnp.where(live_rows[..., None], input_parts[seq_group[:, None], packed_pos], jnp.zeros((), jnp.bfloat16))
    return (outputs, input_grad, totals[0], totals[1], totals[2], totals[3], totals[4], totals[5], totals[6], totals[7], totals[8], totals[9], totals[10], totals[11], totals[12], totals[13], totals[14])
```

```python
import functools

import jax
import jax.numpy as jnp
from jax import lax
from jax.sharding import PartitionSpec as P

HD = 64
EPS = 1e-12
MASKED = -1e9
BF = jnp.bfloat16
F32 = jnp.float32


def dot(a, b):
    return jnp.dot(a, b, preferred_element_type=F32)


def dot_t(a, b):
    return lax.dot_general(a, b, (((1,), (1,)), ((), ())), preferred_element_type=F32)


def t_dot(a, b):
    return lax.dot_general(a, b, (((0,), (0,)), ((), ())), preferred_element_type=F32)


def norm_stats(z):
    c = z - jnp.mean(z, axis=-1, keepdims=True)
    inv = lax.rsqrt(jnp.mean(c * c, axis=-1, keepdims=True) + EPS)
    return c * inv, inv


def norm_back(dy, zhat, inv, gain):
    dg = dy * gain
    m1 = jnp.mean(dg, axis=-1, keepdims=True)
    m2 = jnp.mean(dg * zhat, axis=-1, keepdims=True)
    return inv * (dg - m1 - zhat * m2)


def body(
    inputs,
    cotangent,
    seq_lengths,
    seq_slots,
    offsets,
    query_weight,
    key_weight,
    value_weight,
    query_bias,
    value_bias,
    out_weight,
    out_bias,
    attn_gain,
    attn_shift,
    up_weight,
    up_bias,
    down_weight,
    down_bias,
    ffn_gain,
    ffn_shift,
):
    seqs, rows, width = inputs.shape
    ctx_n = lax.axis_size("ctx")
    fs_n = lax.axis_size("fsdp")
    dev_n = ctx_n * fs_n
    f = lax.axis_index("fsdp")
    c = lax.axis_index("ctx")
    t = lax.axis_index("tp")
    own = width // dev_n
    hcols = query_weight.shape[1]
    heads = hcols // HD
    units = up_weight.shape[1]
    scale = HD ** (-0.5)

    def from_ctx(x, k):
        return x if k == 0 else lax.ppermute(x, "ctx", [(i, i ^ k) for i in range(ctx_n)])

    def from_fsdp(x, j):
        return x if j == 0 else lax.ppermute(x, "fsdp", [(i, (i + j) % fs_n) for i in range(fs_n)])

    def to_fsdp(x, j):
        return x if j == 0 else lax.ppermute(x, "fsdp", [(i, (i - j) % fs_n) for i in range(fs_n)])

    def tp_swap(x):
        return lax.ppermute(x, "tp", [(0, 1), (1, 0)])

    def gather(x):
        plane = jnp.concatenate([from_fsdp(x, j) for j in range(fs_n)], axis=0)
        return jnp.concatenate([from_ctx(plane, k) for k in range(ctx_n)], axis=0)

    def scatter_sum(x):
        per = width // ctx_n
        low = x.astype(BF)
        part = sum(
            from_ctx(low[k * per : (k + 1) * per], k).astype(F32) for k in range(ctx_n)
        )
        low = part.astype(BF)
        return sum(
            to_fsdp(low[j * own : (j + 1) * own], j).astype(F32) for j in range(fs_n)
        )

    rel = jnp.arange(width, dtype=jnp.int32)
    rel_k, rel_j, rel_i = rel // (fs_n * own), rel // own % fs_n, rel % own
    nat = (((f - rel_j) % fs_n) * ctx_n + (c ^ rel_k)) * own + rel_i
    perm = (jnp.arange(width, dtype=jnp.int32)[:, None] == nat[None, :]).astype(BF)
    reld = jnp.arange(dev_n, dtype=jnp.int32)
    dev_of = ((f - reld % fs_n) % fs_n) * ctx_n + (c ^ (reld // fs_n))
    dperm = (jnp.arange(dev_n, dtype=jnp.int32)[:, None] == dev_of[None, :]).astype(F32)

    half = width // 2
    mine = lax.dynamic_slice_in_dim(inputs, t * half, half, axis=2)
    blocks = jnp.stack([from_ctx(mine, k) for k in range(ctx_n)], axis=1)
    other = tp_swap(blocks)
    x_nat = jnp.concatenate(
        [jnp.where(t == 0, blocks, other), jnp.where(t == 0, other, blocks)], axis=-1
    )
    cap = ctx_n * rows
    x_all = dot(x_nat.reshape(seqs * cap, width), perm).astype(BF)
    x_own = x_all.reshape(seqs, ctx_n, rows, width)[:, 0].reshape(seqs * rows, width)
    cot = dot(cotangent.reshape(seqs * rows, width), perm).astype(BF)

    lengths = lax.dynamic_slice_in_dim(seq_lengths, f * seqs, seqs)
    key_pos = (
        (c ^ jnp.arange(ctx_n, dtype=jnp.int32))[:, None] * rows
        + jnp.arange(rows, dtype=jnp.int32)[None, :]
    ).reshape(cap)
    key_live = key_pos[None, :] < lengths[:, None]
    own_live = (c * rows + jnp.arange(rows, dtype=jnp.int32))[None, :] < lengths[:, None]
    live_col = own_live.reshape(seqs * rows, 1)

    vec = jnp.concatenate(
        [
            query_bias.reshape(-1),
            value_bias.reshape(-1),
            out_bias,
            attn_gain,
            attn_shift,
            up_bias.reshape(-1),
            down_bias,
            ffn_gain,
            ffn_shift,
        ]
    )
    vlen = vec.shape[0]
    vrows = -(-vlen // 128)
    vblock = jnp.pad(
        jnp.pad(vec, (0, vrows * 128 - vlen)).reshape(vrows, 128), ((0, own - vrows), (0, 0))
    )
    qkv_all = gather(jnp.concatenate([query_weight, key_weight, value_weight, vblock], axis=1))
    out_all = gather(out_weight.T)
    up_all = gather(up_weight)
    down_all = gather(down_weight.T)
    wq, wkv = qkv_all[:, :hcols], qkv_all[:, hcols : 3 * hcols]
    vecs = (
        qkv_all[:, 3 * hcols :]
        .reshape(dev_n, own, 128)[:, :vrows]
        .reshape(dev_n, vrows * 128)
        .astype(F32)
    )
    qb_n, ub_n = query_bias.shape[1], up_bias.shape[1]
    cuts = [qb_n, qb_n, own, own, own, ub_n, own, own, own]
    at = [sum(cuts[:i]) for i in range(len(cuts))]

    def vec_of(i):
        return vecs[:, at[i] : at[i] + cuts[i]]

    def unit_vec(i):
        return jnp.dot(dperm, vec_of(i), precision=lax.Precision.HIGHEST).reshape(1, -1)

    qb, vb, ub = unit_vec(0), unit_vec(1), unit_vec(5)
    ob, ag, ash, db, fg, fsh = (vec_of(i).reshape(1, width) for i in (2, 3, 4, 6, 7, 8))

    q = (dot(x_own, wq) + qb).astype(BF)
    kv = dot(x_all, wkv)
    keys = kv[:, :hcols].astype(BF)
    values = (kv[:, hcols:] + vb).astype(BF)
    qh = q.reshape(seqs, rows, heads, HD)
    kh = keys.reshape(seqs, cap, heads, HD)
    vh = values.reshape(seqs, cap, heads, HD)
    raw = jnp.einsum("bqhd,bkhd->bhqk", qh, kh, preferred_element_type=F32)
    scores = jnp.where(key_live[:, None, None, :], raw * scale, MASKED)
    top = jnp.max(scores, axis=-1, keepdims=True)
    ex = jnp.exp(scores - top)
    probs = ex / jnp.sum(ex, axis=-1, keepdims=True)
    wts = probs.astype(BF)
    ctxv = (
        jnp.einsum("bhqk,bkhd->bqhd", wts, vh, preferred_element_type=F32)
        .astype(BF)
        .reshape(seqs * rows, hcols)
    )

    def tp_sum(x):
        low = x.astype(BF)
        return low.astype(F32) + tp_swap(low).astype(F32)

    branch = tp_sum(dot_t(ctxv, out_all)) + ob
    hat1, inv1 = norm_stats(x_own.astype(F32) + branch)
    mixed = hat1 * ag + ash
    mixed_low = mixed.astype(BF)
    pre = dot(mixed_low, up_all) + ub
    act = jax.nn.gelu(pre, approximate=False).astype(BF)
    ffn = tp_sum(dot_t(act, down_all)) + db
    hat2, inv2 = norm_stats(mixed + ffn)
    out_rel = (hat2 * fg + fsh).astype(BF)

    dy = jnp.where(live_col, cot, jnp.zeros((), BF)).astype(F32)
    g_fg = jnp.sum(dy * hat2, axis=0)
    g_fs = jnp.sum(dy, axis=0)
    grad_two = norm_back(dy, hat2, inv2, fg)
    ffn_grad = grad_two.astype(BF)
    g_db = jnp.sum(ffn_grad.astype(F32), axis=0)
    g_down = scatter_sum(t_dot(ffn_grad, act))
    act_grad = dot(ffn_grad, down_all)
    _, gelu_back = jax.vjp(functools.partial(jax.nn.gelu, approximate=False), pre)
    up_grad = gelu_back(act_grad)[0].astype(BF)
    g_ub = jnp.sum(up_grad.astype(F32), axis=0)
    g_up = scatter_sum(t_dot(mixed_low, up_grad))
    mixed_grad = grad_two + tp_sum(dot_t(up_grad, up_all))
    g_ag = jnp.sum(mixed_grad * hat1, axis=0)
    g_as = jnp.sum(mixed_grad, axis=0)
    grad_one = norm_back(mixed_grad, hat1, inv1, ag)
    attn_grad = grad_one.astype(BF)
    g_ob = jnp.sum(attn_grad.astype(F32), axis=0)
    g_out = scatter_sum(t_dot(attn_grad, ctxv))
    ctx_grad = dot(attn_grad, out_all).astype(BF)
    cgh = ctx_grad.reshape(seqs, rows, heads, HD)
    pgrad = jnp.einsum("bqhd,bkhd->bhqk", cgh, vh, preferred_element_type=F32)
    delta = jnp.sum(probs * pgrad, axis=-1, keepdims=True)
    sgrad = (probs * (pgrad - delta) * scale).astype(BF)
    dq = (
        jnp.einsum("bhqk,bkhd->bqhd", sgrad, kh, preferred_element_type=F32)
        .astype(BF)
        .reshape(seqs * rows, hcols)
    )
    dk = (
        jnp.einsum("bhqk,bqhd->bkhd", sgrad, qh, preferred_element_type=F32)
        .astype(BF)
        .reshape(seqs * cap, hcols)
    )
    dv = (
        jnp.einsum("bhqk,bqhd->bkhd", wts, cgh, preferred_element_type=F32)
        .astype(BF)
        .reshape(seqs * cap, hcols)
    )
    g_qb = jnp.sum(dq.astype(F32), axis=0)
    g_vb = jnp.sum(dv.astype(F32), axis=0)

    def unit_grad(v):
        return lax.dot_general(
            dperm, v.reshape(dev_n, -1), (((0,), (0,)), ((), ())), precision=lax.Precision.HIGHEST
        )

    vgrads = jnp.concatenate(
        [
            unit_grad(g_qb),
            unit_grad(g_vb),
            g_ob.reshape(dev_n, own),
            g_ag.reshape(dev_n, own),
            g_as.reshape(dev_n, own),
            unit_grad(g_ub),
            g_db.reshape(dev_n, own),
            g_fg.reshape(dev_n, own),
            g_fs.reshape(dev_n, own),
        ],
        axis=1,
    )
    vgrads = jnp.pad(vgrads, ((0, 0), (0, vrows * 128 - vlen))).reshape(dev_n, vrows, 128)
    vgrads = jnp.pad(vgrads, ((0, 0), (0, own - vrows), (0, 0))).reshape(width, 128)
    g_qkv = scatter_sum(
        jnp.concatenate(
            [t_dot(x_own, dq), t_dot(x_all, jnp.concatenate([dk, dv], axis=1)), vgrads], axis=1
        )
    )
    dx = dot_t(jnp.concatenate([dk, dv], axis=1), wkv).reshape(seqs, ctx_n, rows, width)
    dx_own = dot_t(dq, wq) + jnp.where(t == 0, grad_one, 0.0)
    dx = jnp.concatenate(
        [dx[:, :1] + dx_own.reshape(seqs, 1, rows, width), dx[:, 1:]], axis=1
    ).astype(BF)
    back = perm.T
    keep = jnp.where(t == 0, back[:, :half], back[:, half:])
    give = jnp.where(t == 0, back[:, half:], back[:, :half])
    flat = dx.reshape(seqs * cap, width)
    kept = dot(flat, keep) + tp_swap(dot(flat, give).astype(BF)).astype(F32)
    kept = kept.astype(BF).reshape(seqs, ctx_n, rows, half)
    mine = sum(from_ctx(kept[:, k], k).astype(F32) for k in range(ctx_n)).astype(BF)
    other = tp_swap(mine)
    in_grad = jnp.concatenate(
        [jnp.where(t == 0, mine, other), jnp.where(t == 0, other, mine)], axis=-1
    )
    live3 = own_live[:, :, None]
    input_grad = jnp.where(live3, in_grad, jnp.zeros((), BF))
    outputs = jnp.where(
        live3, dot(out_rel, back).astype(BF).reshape(seqs, rows, width), jnp.zeros((), BF)
    )
    gv = g_qkv[:vrows, 3 * hcols :].reshape(-1)

    def own_vec(i):
        return gv[at[i] : at[i] + cuts[i]]

    return (
        outputs,
        input_grad,
        g_qkv[:, :hcols],
        g_qkv[:, hcols : 2 * hcols],
        g_qkv[:, 2 * hcols : 3 * hcols],
        own_vec(0)[None],
        own_vec(1)[None],
        g_out.T,
        own_vec(2),
        own_vec(3),
        own_vec(4),
        g_up,
        own_vec(5)[None],
        g_down.T,
        own_vec(6),
        own_vec(7),
        own_vec(8),
    )


def solution(mesh):
    both = ("fsdp", "ctx")
    rows = P("fsdp", "ctx", None)
    col = P(both, "tp")
    row = P("tp", both)
    vec = P(both)
    params = (col, col, col, row, row, row, vec, vec, vec, col, row, row, vec, vec, vec)
    return jax.shard_map(
        body,
        mesh=mesh,
        in_specs=(rows, rows, P(), P(), P()) + params,
        out_specs=(rows, rows) + params,
        check_vma=False,
    )
```

```python
import functools

import jax
import jax.numpy as jnp
import numpy as np
from jax import lax
from jax.experimental import pallas as pl
from jax.experimental.pallas import tpu as pltpu
from jax.sharding import PartitionSpec as P

HD = 64
EPS = 1e-12
MASKED = -1e9
BF = jnp.bfloat16
F32 = jnp.float32
LANES = 128
ANY = pl.BlockSpec(memory_space=pl.ANY)
SMEM = pl.BlockSpec(memory_space=pltpu.SMEM)
VMEM = pl.BlockSpec(memory_space=pltpu.VMEM)


def dot(a, b):
    return jnp.dot(a, b, preferred_element_type=F32)


def dot_t(a, b):
    return lax.dot_general(a, b, (((1,), (1,)), ((), ())), preferred_element_type=F32)


def t_dot(a, b):
    return lax.dot_general(a, b, (((0,), (0,)), ((), ())), preferred_element_type=F32)


def norm_stats(z):
    c = z - jnp.mean(z, axis=-1, keepdims=True)
    inv = lax.rsqrt(jnp.mean(c * c, axis=-1, keepdims=True) + EPS)
    return c * inv, inv


def norm_back(dy, zhat, inv, gain):
    dg = dy * gain
    m1 = jnp.mean(dg, axis=-1, keepdims=True)
    m2 = jnp.mean(dg * zhat, axis=-1, keepdims=True)
    return inv * (dg - m1 - zhat * m2)


def call(fn, out, ins, args, scratch=(), flops=0, name=None):
    nbytes = sum(a.size * a.dtype.itemsize for a in args)
    nbytes += sum(int(np.prod(s)) * jnp.dtype(d).itemsize for s, d, _ in out)
    return pl.pallas_call(
        fn,
        out_shape=[jax.ShapeDtypeStruct(s, d) for s, d, _ in out],
        in_specs=list(ins),
        out_specs=[s for _, _, s in out],
        scratch_shapes=list(scratch),
        compiler_params=pltpu.CompilerParams(vmem_limit_bytes=60 * 1024 * 1024),
        cost_estimate=pl.CostEstimate(flops=flops, bytes_accessed=nbytes, transcendentals=0),
        name=name,
    )(*args)


def start_all(copies, sems, base=0):
    started = []
    for i, (src, dst) in enumerate(copies):
        cp = pltpu.make_async_copy(src, dst, sems.at[base + i])
        cp.start()
        started.append(cp)
    return started


def wait_all(started):
    for cp in started:
        cp.wait()


def pack_body(wq, wk, wv, ow, vec, up, dn, a, b):
    own, n = wq.shape
    m = up.shape[1]
    r = lax.broadcasted_iota(jnp.int32, (own, own), 0)
    s = lax.broadcasted_iota(jnp.int32, (own, own), 1)
    eye = (r == s).astype(F32).astype(BF)
    a[:, 0:n] = wq[...]
    a[:, n : 2 * n] = wk[...]
    a[:, 2 * n : 3 * n] = wv[...]
    a[:, 3 * n : 4 * n] = dot_t(eye, ow[...]).astype(BF)
    a[:, 4 * n : 4 * n + LANES] = vec[...]
    b[:, 0:m] = up[...]
    b[:, m : 2 * m] = dot_t(eye, dn[...]).astype(BF)


def spread_body(ids, *refs, fs_n, own, cut):
    blocks, (left, right, sems) = refs[:fs_n], refs[fs_n:]
    f = ids[0]
    copies = []
    for j in range(fs_n):
        at = pl.multiple_of(lax.rem(f - j + fs_n, fs_n) * own, 16)
        copies.append((blocks[j].at[:, :cut], left.at[pl.ds(at, own)]))
        copies.append((blocks[j].at[:, cut:], right.at[pl.ds(at, own)]))
    wait_all(start_all(copies, sems))


def load_plane(ids, blocks, dst, sems, base, fs_n, own):
    c = ids[1]
    ctx_n = len(blocks)
    copies = []
    for k in range(ctx_n):
        for g in range(fs_n):
            at = pl.multiple_of((g * ctx_n + (c ^ k)) * own, 16)
            copies.append((blocks[k].at[pl.ds(g * own, own)], dst.at[pl.ds(at, own)]))
    return start_all(copies, sems, base)


def load_rows(ids, blocks, dst, sems, base, seqs, rows):
    c = ids[1]
    ctx_n = len(blocks)
    copies = []
    for k in range(ctx_n):
        for s in range(seqs):
            at = pl.multiple_of(s * ctx_n * rows + (c ^ k) * rows, 16)
            copies.append((blocks[k].at[s], dst.at[pl.ds(at, rows)]))
    return start_all(copies, sems, base)


def store_plane(ids, src, hi, lo, hi_bits, sems, base, fs_n, own, ctx_n):
    c = ids[1]
    copies = []
    n_hi = n_lo = 0
    for k in range(ctx_n):
        for g in range(fs_n):
            at = pl.multiple_of((g * ctx_n + (c ^ k)) * own, 16)
            if k & hi_bits:
                out = hi.at[pl.ds((n_hi * fs_n + g) * own, own)]
            else:
                out = lo.at[pl.ds((n_lo * fs_n + g) * own, own)]
            copies.append((src.at[pl.ds(at, own)], out))
        if k & hi_bits:
            n_hi += 1
        else:
            n_lo += 1
    return start_all(copies, sems, base)


def head_mask(h):
    lane = lax.broadcasted_iota(jnp.int32, (1, LANES), 1)
    return (lane < HD) if h == 0 else (lane >= HD)


def pick(mask, x):
    return jnp.where(mask, x.astype(F32), 0.0).astype(BF)


def softmax_of(qm, kp, live, scale):
    s = jnp.where(live, dot_t(qm, kp) * scale, MASKED)
    e = jnp.exp(s - jnp.max(s, axis=-1, keepdims=True))
    return e / jnp.sum(e, axis=-1, keepdims=True)


def attn_body(
    ids, lens, xo, x1, x2, x3, l0, l1, l2, l3, r0, r1, r2, r3, vsel, mod_q, base_q, mod_w, base_w, mod_u, base_u,
    branch, q_o, k_o, v_o, ctx_o, vw_o, vu_o,
    xs, wl, wr, sems, *, fs_n, own, seqs, rows, dev_n,
):
    ctx_n = 4
    hcols = q_o.shape[1]
    cap = ctx_n * rows
    xcp = load_rows(ids, (xo, x1, x2, x3), xs, sems, 0, seqs, rows)
    wcp = load_plane(ids, (l0, l1, l2, l3), wl, sems, ctx_n * seqs, fs_n, own)
    wcp += load_plane(ids, (r0, r1, r2, r3), wr, sems, ctx_n * (seqs + fs_n), fs_n, own)
    wait_all(xcp + wcp)
    vv = dot(vsel[...], wr[:, 2 * hcols : 2 * hcols + LANES]).astype(BF)

    def unpack(i, mod, base):
        n = mod.shape[1]
        lane = lax.broadcasted_iota(jnp.int32, (LANES, n), 0)
        sel = (lane == mod[...]).astype(F32).astype(BF)
        t = dot(vv[i * dev_n : (i + 1) * dev_n], sel)
        dev = lax.broadcasted_iota(jnp.int32, (dev_n, n), 0)
        return jnp.sum(jnp.where(dev == base[...], t, 0.0), axis=0, keepdims=True)

    qb = unpack(0, mod_q, base_q)
    vb = unpack(1, mod_q, base_q)
    for row, i in enumerate((2, 3, 4, 6, 7, 8)):
        vw_o[row : row + 1, :] = unpack(i, mod_w, base_w)
    vu_o[0:1, :] = unpack(5, mod_u, base_u)

    scale = HD**-0.5
    x_own = xo[...].reshape(seqs * rows, xo.shape[2])
    q_o[...] = (dot(x_own, wl[:, :hcols]) + qb).astype(BF)
    for s in range(seqs):
        part = pl.ds(s * cap, cap)
        k_o[part, :] = dot(xs[part, :], wl[:, hcols : 2 * hcols]).astype(BF)
        v_o[part, :] = (dot(xs[part, :], wr[:, :hcols]) + vb).astype(BF)
    for s in range(seqs):
        live = lax.broadcasted_iota(jnp.int32, (1, cap), 1) < lens[s]
        for p in range(hcols // LANES):
            cols = slice(p * LANES, (p + 1) * LANES)
            qp = q_o[s * rows : (s + 1) * rows, cols]
            kp = k_o[s * cap : (s + 1) * cap, cols]
            vp = v_o[s * cap : (s + 1) * cap, cols]
            acc = jnp.zeros((rows, LANES), F32)
            for h in range(LANES // HD):
                mask = head_mask(h)
                w = softmax_of(pick(mask, qp), kp, live, scale).astype(BF)
                acc = jnp.where(mask, dot(w, vp), acc)
            ctx_o[s * rows : (s + 1) * rows, cols] = acc.astype(BF)
    branch[...] = dot_t(ctx_o[...], wr[:, hcols : 2 * hcols]).astype(BF)


def up_body(ids, x, low, other, vw, vu, u0, u1, u2, u3, hat_o, inv_o, ml_o, pre_o, act_o, w, sems, *, fs_n, own):
    cp = load_plane(ids, (u0, u1, u2, u3), w, sems, 0, fs_n, own)
    z = x[...].astype(F32) + low[...].astype(F32) + other[...].astype(F32) + vw[0:1, :]
    hat, inv = norm_stats(z)
    hat_o[...] = hat
    inv_o[...] = inv
    ml_o[...] = (hat * vw[1:2, :] + vw[2:3, :]).astype(BF)
    wait_all(cp)
    units = w.shape[1]
    step = 512
    for i in range(units // step):
        cols = slice(i * step, (i + 1) * step)
        pre = dot(ml_o[...], w[:, cols]) + vu[0:1, cols]
        pre_o[:, cols] = pre
        act_o[:, cols] = (pre * (0.5 + 0.5 * lax.erf(pre * (0.5**0.5)))).astype(BF)


def down_body(ids, act, d0, d1, d2, d3, out, w, sems, *, fs_n, own):
    wait_all(load_plane(ids, (d0, d1, d2, d3), w, sems, 0, fs_n, own))
    out[...] = dot_t(act[...], w[...]).astype(BF)


def ffn_back_body(
    ids, lens, hat1, low, other, vw, cot, pre, u0, u1, u2, u3, d0, d1, d2, d3,
    out_o, g2_o, fg_o, ug_o, dm_o, gw_o, gu_o,
    wu, wd, sems, *, fs_n, own, rows, seqs,
):
    c = ids[1]
    dcp = load_plane(ids, (d0, d1, d2, d3), wd, sems, 0, fs_n, own)
    ucp = load_plane(ids, (u0, u1, u2, u3), wu, sems, 4 * fs_n, fs_n, own)
    hat = hat1[...]
    z = hat * vw[1:2, :] + vw[2:3, :] + low[...].astype(F32) + other[...].astype(F32) + vw[3:4, :]
    hat2, inv2 = norm_stats(z)
    pos = c * rows + lax.broadcasted_iota(jnp.int32, (rows, 1), 0)
    live = jnp.concatenate([(pos < lens[s]).astype(F32) for s in range(seqs)], axis=0) > 0.5
    out_o[...] = jnp.where(live, hat2 * vw[4:5, :] + vw[5:6, :], 0.0).astype(BF)
    dy = jnp.where(live, cot[...].astype(F32), 0.0)
    g2 = norm_back(dy, hat2, inv2, vw[4:5, :])
    g2_o[...] = g2
    fg_o[...] = g2.astype(BF)
    gw_o[0:1, :] = jnp.sum(g2.astype(BF).astype(F32), axis=0, keepdims=True)
    gw_o[1:2, :] = jnp.sum(dy * hat2, axis=0, keepdims=True)
    gw_o[2:3, :] = jnp.sum(dy, axis=0, keepdims=True)
    wait_all(dcp)
    units = wu.shape[1]
    step = 512
    for i in range(units // step):
        cols = slice(i * step, (i + 1) * step)
        ag = dot(fg_o[...], wd[:, cols])
        u = pre[:, cols]
        phi = 0.5 + 0.5 * lax.erf(u * (0.5**0.5))
        grad = (ag * (phi + u * jnp.exp(-0.5 * u * u) * 0.3989422804014327)).astype(BF)
        ug_o[:, cols] = grad
        gu_o[0:1, cols] = jnp.sum(grad.astype(F32), axis=0, keepdims=True)
    wait_all(ucp)
    dm_o[...] = dot_t(ug_o[...], wu[...]).astype(BF)


def ffn_grads_body(ids, ml, ug, fg, act, uh, ulo, dh, dlo, gu, gd, sems, *, fs_n, own):
    ctx_n = 4
    units = gu.shape[1]
    step = 512
    for i in range(units // step):
        cols = slice(i * step, (i + 1) * step)
        gu[:, cols] = t_dot(ml[...], ug[:, cols]).astype(BF)
    cps = store_plane(ids, gu, uh, ulo, 2, sems, 0, fs_n, own, ctx_n)
    for i in range(units // step):
        cols = slice(i * step, (i + 1) * step)
        gd[:, cols] = t_dot(fg[...], act[:, cols]).astype(BF)
    cps += store_plane(ids, gd, dh, dlo, 1, sems, ctx_n * fs_n, fs_n, own, ctx_n)
    wait_all(cps)


def attn_back_body(
    ids, lens, hat1, inv1, vw, g2, low, other, xo, x1, x2, x3, r0, r1, r2, r3, q, k, v, ctx, gw, gu,
    vsel, mod_q, base_q, mod_w, base_w, mod_u, base_u,
    lh, llo, rh, rlo, g1_o, dq_o, dk_o, dv_o,
    xs, wr, gl, gr, vg, sems, *, fs_n, own, seqs, rows, dev_n,
):
    ctx_n = 4
    hcols = q.shape[1]
    cap = ctx_n * rows
    wcp = load_plane(ids, (r0, r1, r2, r3), wr, sems, 0, fs_n, own)
    xcp = load_rows(ids, (xo, x1, x2, x3), xs, sems, ctx_n * fs_n, seqs, rows)
    hat = hat1[...]
    mg = g2[...] + low[...].astype(F32) + other[...].astype(F32)
    g1 = norm_back(mg, hat, inv1[...], vw[1:2, :])
    g1_o[...] = g1
    ag = g1.astype(BF)
    wait_all(wcp)
    cg = dot(ag, wr[:, hcols : 2 * hcols]).astype(BF)
    scale = HD**-0.5
    for s in range(seqs):
        live = lax.broadcasted_iota(jnp.int32, (1, cap), 1) < lens[s]
        for p in range(hcols // LANES):
            cols = slice(p * LANES, (p + 1) * LANES)
            qp = q[s * rows : (s + 1) * rows, cols]
            kp = k[s * cap : (s + 1) * cap, cols]
            vp = v[s * cap : (s + 1) * cap, cols]
            cp = cg[s * rows : (s + 1) * rows, cols]
            dq = jnp.zeros((rows, LANES), F32)
            dk = jnp.zeros((cap, LANES), F32)
            dv = jnp.zeros((cap, LANES), F32)
            for h in range(LANES // HD):
                mask = head_mask(h)
                qm = pick(mask, qp)
                cm = pick(mask, cp)
                probs = softmax_of(qm, kp, live, scale)
                pg = dot_t(cm, vp)
                delta = jnp.sum(probs * pg, axis=-1, keepdims=True)
                sg = (probs * (pg - delta) * scale).astype(BF)
                dq = jnp.where(mask, dot(sg, kp), dq)
                dk = dk + t_dot(sg, qm)
                dv = dv + t_dot(probs.astype(BF), cm)
            dq_o[s * rows : (s + 1) * rows, cols] = dq.astype(BF)
            dk_o[s * cap : (s + 1) * cap, cols] = dk.astype(BF)
            dv_o[s * cap : (s + 1) * cap, cols] = dv.astype(BF)
    wait_all(xcp)
    x_own = xo[...].reshape(seqs * rows, xo.shape[2])
    gl[:, :hcols] = t_dot(x_own, dq_o[...]).astype(BF)
    gl[:, hcols:] = t_dot(xs[...], dk_o[...]).astype(BF)
    cps = store_plane(ids, gl, lh, llo, 2, sems, 0, fs_n, own, ctx_n)
    gr[:, :hcols] = t_dot(xs[...], dv_o[...]).astype(BF)
    gr[:, hcols : 2 * hcols] = t_dot(ag, ctx[...]).astype(BF)

    def pack(i, g, mod, base):
        n = mod.shape[1]
        lane = lax.broadcasted_iota(jnp.int32, (LANES, n), 0)
        sel = (lane == mod[...]).astype(F32).astype(BF)
        dev = lax.broadcasted_iota(jnp.int32, (dev_n, n), 0)
        rowsel = jnp.where(dev == base[...], g, 0.0).astype(BF)
        vg[i * dev_n : (i + 1) * dev_n, :] = dot_t(rowsel, sel).astype(BF)

    def total(x):
        return jnp.sum(x.astype(F32), axis=0, keepdims=True)

    pack(0, total(dq_o[...]), mod_q, base_q)
    pack(1, total(dv_o[...]), mod_q, base_q)
    pack(2, total(ag), mod_w, base_w)
    pack(3, total(mg * hat), mod_w, base_w)
    pack(4, total(mg), mod_w, base_w)
    pack(5, gu[0:1, :], mod_u, base_u)
    for i in range(3):
        pack(6 + i, gw[i : i + 1, :], mod_w, base_w)
    gr[:, 2 * hcols :] = t_dot(vsel[...], vg[...]).astype(BF)
    cps += store_plane(ids, gr, rh, rlo, 1, sems, 4 * fs_n, fs_n, own, ctx_n)
    wait_all(cps)


def dx_body(
    ids, g1, dq, dk, dv, l0, l1, l2, l3, r0, r1, r2, r3, keep_o, give_o, wl, wr, acc, sems, *, fs_n, own, seqs, rows
):
    ctx_n = 4
    hcols = dq.shape[1]
    cap = ctx_n * rows
    width = wl.shape[0]
    half = width // 2
    cp = load_plane(ids, (l0, l1, l2, l3), wl, sems, 0, fs_n, own)
    cp += load_plane(ids, (r0, r1, r2, r3), wr, sems, ctx_n * fs_n, fs_n, own)
    c, t = ids[1], ids[2]
    wait_all(cp)
    for s in range(seqs):
        part = slice(s * cap, (s + 1) * cap)
        acc[part, :] = dot_t(dk[part, :], wl[:, hcols : 2 * hcols]) + dot_t(dv[part, :], wr[:, :hcols])
    own_part = dot_t(dq[...], wl[:, :hcols]) + jnp.where(t == 0, g1[...], 0.0)
    for s in range(seqs):
        at = pl.ds(pl.multiple_of(s * cap + c * rows, 16), rows)
        acc[at, :] = acc[at, :] + own_part[s * rows : (s + 1) * rows]
    first = acc[:, :half].astype(BF)
    second = acc[:, half:].astype(BF)
    low = t == 0
    keep_o[...] = jnp.where(low, first.astype(F32), second.astype(F32)).astype(BF)
    give_o[...] = jnp.where(low, second.astype(F32), first.astype(F32)).astype(BF)


def fast_body(
    inputs, cotangent, seq_lengths, seq_slots, offsets,
    query_weight, key_weight, value_weight, query_bias, value_bias, out_weight, out_bias,
    attn_gain, attn_shift, up_weight, up_bias, down_weight, down_bias, ffn_gain, ffn_shift,
):
    seqs, rows, width = inputs.shape
    ctx_n = lax.axis_size("ctx")
    fs_n = lax.axis_size("fsdp")
    dev_n = ctx_n * fs_n
    f = lax.axis_index("fsdp")
    c = lax.axis_index("ctx")
    t = lax.axis_index("tp")
    own = width // dev_n
    hcols = query_weight.shape[1]
    units = up_weight.shape[1]
    toks = seqs * rows
    cap = ctx_n * rows
    n_left, n_right = 2 * hcols, 2 * hcols + LANES
    ids = jnp.stack([f, c, t]).astype(jnp.int32)
    lens = lax.dynamic_slice_in_dim(seq_lengths, f * seqs, seqs)
    dma = lambda n: pltpu.SemaphoreType.DMA((n,))

    def from_ctx(x, k):
        return lax.ppermute(x, "ctx", [(i, i ^ k) for i in range(ctx_n)])

    def from_fsdp(x, j):
        return lax.ppermute(x, "fsdp", [(i, (i + j) % fs_n) for i in range(fs_n)])

    def to_fsdp(x, j):
        return lax.ppermute(x, "fsdp", [(i, (i - j) % fs_n) for i in range(fs_n)])

    def tp_swap(x):
        return lax.ppermute(x, "tp", [(0, 1), (1, 0)])

    def after(x, *deps):
        return lax.optimization_barrier((x,) + deps)[0]

    def table(n):
        m = np.arange(dev_n * n, dtype=np.int32)
        return jnp.asarray(m % n)[None], jnp.asarray(m // n)[None]

    mod_q, base_q = table(query_bias.shape[1])
    mod_w, base_w = table(own)
    mod_u, base_u = table(up_bias.shape[1])
    n_vec = 9
    sel = np.zeros((n_vec * dev_n, width), np.float32)
    for i in range(n_vec):
        for d in range(dev_n):
            sel[i * dev_n + d, d * own + i] = 1
    vsel = jnp.asarray(sel, BF)
    tables = (vsel, mod_q, base_q, mod_w, base_w, mod_u, base_u)

    vecs = (query_bias, value_bias, out_bias, attn_gain, attn_shift, up_bias, down_bias, ffn_gain, ffn_shift)
    vec = jnp.stack([jnp.pad(v.reshape(-1), (0, LANES - v.size)) for v in vecs])
    vec = jnp.pad(vec, ((0, own - n_vec), (0, 0)))

    xr = [from_ctx(inputs, k) for k in range(1, ctx_n)]

    msg_a, msg_b = call(
        pack_body,
        [((own, n_left + n_right), BF, VMEM), ((own, 2 * units), BF, VMEM)],
        [VMEM] * 7,
        (query_weight, key_weight, value_weight, out_weight, vec, up_weight, down_weight),
        name="pack",
    )

    def spread(msg, blocks, cut, name):
        n = msg.shape[1]
        return call(
            functools.partial(spread_body, fs_n=fs_n, own=own, cut=cut),
            [((fs_n * own, cut), BF, ANY), ((fs_n * own, n - cut), BF, ANY)],
            [SMEM] + [ANY] * fs_n,
            (ids, msg, *blocks),
            scratch=[dma(2 * fs_n)],
            name=name,
        )

    def plane(left, right):
        l1, l2 = from_ctx(left, 1), from_ctx(left, 2)
        r2, r1 = from_ctx(right, 2), from_ctx(right, 1)
        l3 = from_ctx(l1, 2)
        r3 = from_ctx(r2, 1)
        return (left, l1, l2, l3), (right, r1, r2, r3)

    za = [from_fsdp(msg_a, j) for j in range(1, fs_n)]
    zb_in = after(msg_b, *za)
    zb = [from_fsdp(zb_in, j) for j in range(1, fs_n)]
    left, right = plane(*spread(msg_a, za, n_left, "spread_a"))
    up_z, dn_z = spread(msg_b, zb, units, "spread_b")
    up_z = after(up_z, left[3], right[3])
    dn_z = after(dn_z, left[3], right[3])
    up_w, dn_w = plane(up_z, dn_z)

    x_blocks = (inputs, *xr)
    sizes = dict(fs_n=fs_n, own=own)
    branch, q, k, v, ctx, vw, vu = call(
        functools.partial(attn_body, seqs=seqs, rows=rows, dev_n=dev_n, **sizes),
        [
            ((toks, width), BF, VMEM),
            ((toks, hcols), BF, VMEM),
            ((seqs * cap, hcols), BF, VMEM),
            ((seqs * cap, hcols), BF, VMEM),
            ((toks, hcols), BF, VMEM),
            ((8, width), F32, VMEM),
            ((8, units), F32, VMEM),
        ],
        [SMEM, SMEM, VMEM] + [ANY] * 11 + [VMEM] * 7,
        (ids, lens, *x_blocks, *left, *right, *tables),
        scratch=[
            pltpu.VMEM((seqs * cap, width), BF),
            pltpu.VMEM((width, n_left), BF),
            pltpu.VMEM((width, n_right), BF),
            dma(ctx_n * (seqs + 2 * fs_n)),
        ],
        flops=4 * 10**9,
        name="attention",
    )
    x_own = inputs.reshape(toks, width)
    hat1, inv1, mixed_low, pre, act = call(
        functools.partial(up_body, **sizes),
        [
            ((toks, width), F32, VMEM),
            ((toks, 1), F32, VMEM),
            ((toks, width), BF, VMEM),
            ((toks, units), F32, VMEM),
            ((toks, units), BF, VMEM),
        ],
        [SMEM] + [VMEM] * 5 + [ANY] * 4,
        (ids, x_own, branch, tp_swap(branch), vw, vu, *up_w),
        scratch=[pltpu.VMEM((width, units), BF), dma(ctx_n * fs_n)],
        flops=2 * 10**9,
        name="up",
    )
    (ffn,) = call(
        functools.partial(down_body, **sizes),
        [((toks, width), BF, VMEM)],
        [SMEM, VMEM] + [ANY] * 4,
        (ids, act, *dn_w),
        scratch=[pltpu.VMEM((width, units), BF), dma(ctx_n * fs_n)],
        flops=10**9,
        name="down",
    )
    outputs, grad_two, ffn_grad, up_grad, dmix, gw, gu = call(
        functools.partial(ffn_back_body, rows=rows, seqs=seqs, **sizes),
        [
            ((toks, width), BF, VMEM),
            ((toks, width), F32, VMEM),
            ((toks, width), BF, VMEM),
            ((toks, units), BF, VMEM),
            ((toks, width), BF, VMEM),
            ((8, width), F32, VMEM),
            ((8, units), F32, VMEM),
        ],
        [SMEM, SMEM] + [VMEM] * 6 + [ANY] * 8,
        (ids, lens, hat1, ffn, tp_swap(ffn), vw, cotangent.reshape(toks, width), pre, *up_w, *dn_w),
        scratch=[
            pltpu.VMEM((width, units), BF),
            pltpu.VMEM((width, units), BF),
            dma(2 * ctx_n * fs_n),
        ],
        flops=4 * 10**9,
        name="ffn_back",
    )
    dmix_other = tp_swap(dmix)
    blk = fs_n * own
    uh, ulo, dh, dlo = call(
        functools.partial(ffn_grads_body, **sizes),
        [((2 * blk, units), BF, ANY)] * 4,
        [SMEM] + [VMEM] * 4,
        (ids, mixed_low, up_grad, ffn_grad, act),
        scratch=[
            pltpu.VMEM((width, units), BF),
            pltpu.VMEM((width, units), BF),
            dma(2 * ctx_n * fs_n),
        ],
        flops=4 * 10**9,
        name="ffn_grads",
    )

    def plane_sum(lh, llo, rh, rlo):
        def one(hi, lo, first, second):
            got = from_ctx(hi, first)
            send = (lo[blk:].astype(F32) + got[blk:].astype(F32)).astype(BF)
            got2 = from_ctx(send, second)
            return (lo[:blk].astype(F32) + got[:blk].astype(F32) + got2.astype(F32)).astype(BF)

        return one(lh, llo, 2, 1), one(rh, rlo, 1, 2)

    def z_sum(*arrays):
        low = jnp.concatenate(arrays, axis=1)
        total = lax.dynamic_slice_in_dim(low, f * own, own).astype(F32)
        for j in range(1, fs_n):
            piece = lax.dynamic_slice_in_dim(low, lax.rem(f - j + fs_n, fs_n) * own, own)
            total = total + to_fsdp(piece, j).astype(F32)
        return total

    g_ffn = z_sum(*plane_sum(uh, ulo, dh, dlo))

    lh, llo, rh, rlo, grad_one, dq, dk, dv = call(
        functools.partial(attn_back_body, seqs=seqs, rows=rows, dev_n=dev_n, **sizes),
        [
            ((2 * blk, n_left), BF, ANY),
            ((2 * blk, n_left), BF, ANY),
            ((2 * blk, n_right), BF, ANY),
            ((2 * blk, n_right), BF, ANY),
            ((toks, width), F32, VMEM),
            ((toks, hcols), BF, VMEM),
            ((seqs * cap, hcols), BF, VMEM),
            ((seqs * cap, hcols), BF, VMEM),
        ],
        [SMEM, SMEM] + [VMEM] * 7 + [ANY] * 7 + [VMEM] * 13,
        (
            ids, lens, hat1, inv1, vw, grad_two, dmix, dmix_other, *x_blocks, *right, q, k, v, ctx, gw, gu, *tables,
        ),
        scratch=[
            pltpu.VMEM((seqs * cap, width), BF),
            pltpu.VMEM((width, n_right), BF),
            pltpu.VMEM((width, n_left), BF),
            pltpu.VMEM((width, n_right), BF),
            pltpu.VMEM((n_vec * dev_n, LANES), BF),
            dma(ctx_n * (2 * fs_n + seqs)),
        ],
        flops=6 * 10**9,
        name="attention_back",
    )
    g_attn = z_sum(*plane_sum(lh, llo, rh, rlo))

    half = width // 2
    keep, give = call(
        functools.partial(dx_body, seqs=seqs, rows=rows, **sizes),
        [((seqs * cap, half), BF, VMEM)] * 2,
        [SMEM] + [VMEM] * 4 + [ANY] * 8,
        (ids, grad_one, dq, dk, dv, *left, *right),
        scratch=[
            pltpu.VMEM((width, n_left), BF),
            pltpu.VMEM((width, n_right), BF),
            pltpu.VMEM((seqs * cap, width), F32),
            dma(2 * ctx_n * fs_n),
        ],
        flops=3 * 10**9,
        name="input_grad",
    )
    both = keep.astype(F32) + tp_swap(give).astype(F32)
    both = both.astype(BF).reshape(seqs, ctx_n, rows, half)
    mine = lax.dynamic_index_in_dim(both, c, 1, keepdims=False).astype(F32)
    for j in range(1, ctx_n):
        piece = lax.dynamic_index_in_dim(both, c ^ j, 1, keepdims=False)
        mine = mine + from_ctx(piece, j).astype(F32)
    mine = mine.astype(BF)
    theirs = tp_swap(mine)
    in_grad = jnp.concatenate(
        [jnp.where(t == 0, mine, theirs), jnp.where(t == 0, theirs, mine)], axis=-1
    )
    own_live = (c * rows + jnp.arange(rows, dtype=jnp.int32))[None, :] < lens[:, None]
    input_grad = jnp.where(own_live[:, :, None], in_grad, jnp.zeros((), BF))

    gv = g_attn[:n_vec, 4 * hcols :]

    def own_vec(i, n):
        return gv[i, :n]

    qb_n, ub_n = query_bias.shape[1], up_bias.shape[1]
    return (
        outputs.reshape(seqs, rows, width),
        input_grad,
        g_attn[:, :hcols],
        g_attn[:, hcols : 2 * hcols],
        g_attn[:, 2 * hcols : 3 * hcols],
        own_vec(0, qb_n)[None],
        own_vec(1, qb_n)[None],
        g_attn[:, 3 * hcols : 4 * hcols].T,
        own_vec(2, own),
        own_vec(3, own),
        own_vec(4, own),
        g_ffn[:, :units],
        own_vec(5, ub_n)[None],
        g_ffn[:, units:].T,
        own_vec(6, own),
        own_vec(7, own),
        own_vec(8, own),
    )


def general_body(
    inputs,
    cotangent,
    seq_lengths,
    seq_slots,
    offsets,
    query_weight,
    key_weight,
    value_weight,
    query_bias,
    value_bias,
    out_weight,
    out_bias,
    attn_gain,
    attn_shift,
    up_weight,
    up_bias,
    down_weight,
    down_bias,
    ffn_gain,
    ffn_shift,
):
    seqs, rows, width = inputs.shape
    ctx_n = lax.axis_size("ctx")
    fs_n = lax.axis_size("fsdp")
    dev_n = ctx_n * fs_n
    f = lax.axis_index("fsdp")
    c = lax.axis_index("ctx")
    t = lax.axis_index("tp")
    own = width // dev_n
    hcols = query_weight.shape[1]
    heads = hcols // HD
    units = up_weight.shape[1]
    scale = HD ** (-0.5)

    def from_ctx(x, k):
        return x if k == 0 else lax.ppermute(x, "ctx", [(i, i ^ k) for i in range(ctx_n)])

    def from_fsdp(x, j):
        return x if j == 0 else lax.ppermute(x, "fsdp", [(i, (i + j) % fs_n) for i in range(fs_n)])

    def to_fsdp(x, j):
        return x if j == 0 else lax.ppermute(x, "fsdp", [(i, (i - j) % fs_n) for i in range(fs_n)])

    def tp_swap(x):
        return lax.ppermute(x, "tp", [(0, 1), (1, 0)])

    def gather(x):
        plane = jnp.concatenate([from_fsdp(x, j) for j in range(fs_n)], axis=0)
        return jnp.concatenate([from_ctx(plane, k) for k in range(ctx_n)], axis=0)

    def scatter_sum(x):
        per = width // ctx_n
        low = x.astype(BF)
        part = sum(
            from_ctx(low[k * per : (k + 1) * per], k).astype(F32) for k in range(ctx_n)
        )
        low = part.astype(BF)
        return sum(
            to_fsdp(low[j * own : (j + 1) * own], j).astype(F32) for j in range(fs_n)
        )

    rel = jnp.arange(width, dtype=jnp.int32)
    rel_k, rel_j, rel_i = rel // (fs_n * own), rel // own % fs_n, rel % own
    nat = (((f - rel_j) % fs_n) * ctx_n + (c ^ rel_k)) * own + rel_i
    perm = (jnp.arange(width, dtype=jnp.int32)[:, None] == nat[None, :]).astype(BF)
    reld = jnp.arange(dev_n, dtype=jnp.int32)
    dev_of = ((f - reld % fs_n) % fs_n) * ctx_n + (c ^ (reld // fs_n))
    dperm = (jnp.arange(dev_n, dtype=jnp.int32)[:, None] == dev_of[None, :]).astype(F32)

    half = width // 2
    mine = lax.dynamic_slice_in_dim(inputs, t * half, half, axis=2)
    blocks = jnp.stack([from_ctx(mine, k) for k in range(ctx_n)], axis=1)
    other = tp_swap(blocks)
    x_nat = jnp.concatenate(
        [jnp.where(t == 0, blocks, other), jnp.where(t == 0, other, blocks)], axis=-1
    )
    cap = ctx_n * rows
    x_all = dot(x_nat.reshape(seqs * cap, width), perm).astype(BF)
    x_own = x_all.reshape(seqs, ctx_n, rows, width)[:, 0].reshape(seqs * rows, width)
    cot = dot(cotangent.reshape(seqs * rows, width), perm).astype(BF)

    lengths = lax.dynamic_slice_in_dim(seq_lengths, f * seqs, seqs)
    key_pos = (
        (c ^ jnp.arange(ctx_n, dtype=jnp.int32))[:, None] * rows
        + jnp.arange(rows, dtype=jnp.int32)[None, :]
    ).reshape(cap)
    key_live = key_pos[None, :] < lengths[:, None]
    own_live = (c * rows + jnp.arange(rows, dtype=jnp.int32))[None, :] < lengths[:, None]
    live_col = own_live.reshape(seqs * rows, 1)

    vec = jnp.concatenate(
        [
            query_bias.reshape(-1),
            value_bias.reshape(-1),
            out_bias,
            attn_gain,
            attn_shift,
            up_bias.reshape(-1),
            down_bias,
            ffn_gain,
            ffn_shift,
        ]
    )
    vlen = vec.shape[0]
    vrows = -(-vlen // 128)
    vblock = jnp.pad(
        jnp.pad(vec, (0, vrows * 128 - vlen)).reshape(vrows, 128), ((0, own - vrows), (0, 0))
    )
    qkv_all = gather(jnp.concatenate([query_weight, key_weight, value_weight, vblock], axis=1))
    out_all = gather(out_weight.T)
    up_all = gather(up_weight)
    down_all = gather(down_weight.T)
    wq, wkv = qkv_all[:, :hcols], qkv_all[:, hcols : 3 * hcols]
    vecs = (
        qkv_all[:, 3 * hcols :]
        .reshape(dev_n, own, 128)[:, :vrows]
        .reshape(dev_n, vrows * 128)
        .astype(F32)
    )
    qb_n, ub_n = query_bias.shape[1], up_bias.shape[1]
    cuts = [qb_n, qb_n, own, own, own, ub_n, own, own, own]
    at = [sum(cuts[:i]) for i in range(len(cuts))]

    def vec_of(i):
        return vecs[:, at[i] : at[i] + cuts[i]]

    def unit_vec(i):
        return jnp.dot(dperm, vec_of(i), precision=lax.Precision.HIGHEST).reshape(1, -1)

    qb, vb, ub = unit_vec(0), unit_vec(1), unit_vec(5)
    ob, ag, ash, db, fg, fsh = (vec_of(i).reshape(1, width) for i in (2, 3, 4, 6, 7, 8))

    q = (dot(x_own, wq) + qb).astype(BF)
    kv = dot(x_all, wkv)
    keys = kv[:, :hcols].astype(BF)
    values = (kv[:, hcols:] + vb).astype(BF)
    qh = q.reshape(seqs, rows, heads, HD)
    kh = keys.reshape(seqs, cap, heads, HD)
    vh = values.reshape(seqs, cap, heads, HD)
    raw = jnp.einsum("bqhd,bkhd->bhqk", qh, kh, preferred_element_type=F32)
    scores = jnp.where(key_live[:, None, None, :], raw * scale, MASKED)
    top = jnp.max(scores, axis=-1, keepdims=True)
    ex = jnp.exp(scores - top)
    probs = ex / jnp.sum(ex, axis=-1, keepdims=True)
    wts = probs.astype(BF)
    ctxv = (
        jnp.einsum("bhqk,bkhd->bqhd", wts, vh, preferred_element_type=F32)
        .astype(BF)
        .reshape(seqs * rows, hcols)
    )

    def tp_sum(x):
        low = x.astype(BF)
        return low.astype(F32) + tp_swap(low).astype(F32)

    branch = tp_sum(dot_t(ctxv, out_all)) + ob
    hat1, inv1 = norm_stats(x_own.astype(F32) + branch)
    mixed = hat1 * ag + ash
    mixed_low = mixed.astype(BF)
    pre = dot(mixed_low, up_all) + ub
    act = jax.nn.gelu(pre, approximate=False).astype(BF)
    ffn = tp_sum(dot_t(act, down_all)) + db
    hat2, inv2 = norm_stats(mixed + ffn)
    out_rel = (hat2 * fg + fsh).astype(BF)

    dy = jnp.where(live_col, cot, jnp.zeros((), BF)).astype(F32)
    g_fg = jnp.sum(dy * hat2, axis=0)
    g_fs = jnp.sum(dy, axis=0)
    grad_two = norm_back(dy, hat2, inv2, fg)
    ffn_grad = grad_two.astype(BF)
    g_db = jnp.sum(ffn_grad.astype(F32), axis=0)
    g_down = scatter_sum(t_dot(ffn_grad, act))
    act_grad = dot(ffn_grad, down_all)
    _, gelu_back = jax.vjp(functools.partial(jax.nn.gelu, approximate=False), pre)
    up_grad = gelu_back(act_grad)[0].astype(BF)
    g_ub = jnp.sum(up_grad.astype(F32), axis=0)
    g_up = scatter_sum(t_dot(mixed_low, up_grad))
    mixed_grad = grad_two + tp_sum(dot_t(up_grad, up_all))
    g_ag = jnp.sum(mixed_grad * hat1, axis=0)
    g_as = jnp.sum(mixed_grad, axis=0)
    grad_one = norm_back(mixed_grad, hat1, inv1, ag)
    attn_grad = grad_one.astype(BF)
    g_ob = jnp.sum(attn_grad.astype(F32), axis=0)
    g_out = scatter_sum(t_dot(attn_grad, ctxv))
    ctx_grad = dot(attn_grad, out_all).astype(BF)
    cgh = ctx_grad.reshape(seqs, rows, heads, HD)
    pgrad = jnp.einsum("bqhd,bkhd->bhqk", cgh, vh, preferred_element_type=F32)
    delta = jnp.sum(probs * pgrad, axis=-1, keepdims=True)
    sgrad = (probs * (pgrad - delta) * scale).astype(BF)
    dq = (
        jnp.einsum("bhqk,bkhd->bqhd", sgrad, kh, preferred_element_type=F32)
        .astype(BF)
        .reshape(seqs * rows, hcols)
    )
    dk = (
        jnp.einsum("bhqk,bqhd->bkhd", sgrad, qh, preferred_element_type=F32)
        .astype(BF)
        .reshape(seqs * cap, hcols)
    )
    dv = (
        jnp.einsum("bhqk,bqhd->bkhd", wts, cgh, preferred_element_type=F32)
        .astype(BF)
        .reshape(seqs * cap, hcols)
    )
    g_qb = jnp.sum(dq.astype(F32), axis=0)
    g_vb = jnp.sum(dv.astype(F32), axis=0)

    def unit_grad(v):
        return lax.dot_general(
            dperm, v.reshape(dev_n, -1), (((0,), (0,)), ((), ())), precision=lax.Precision.HIGHEST
        )

    vgrads = jnp.concatenate(
        [
            unit_grad(g_qb),
            unit_grad(g_vb),
            g_ob.reshape(dev_n, own),
            g_ag.reshape(dev_n, own),
            g_as.reshape(dev_n, own),
            unit_grad(g_ub),
            g_db.reshape(dev_n, own),
            g_fg.reshape(dev_n, own),
            g_fs.reshape(dev_n, own),
        ],
        axis=1,
    )
    vgrads = jnp.pad(vgrads, ((0, 0), (0, vrows * 128 - vlen))).reshape(dev_n, vrows, 128)
    vgrads = jnp.pad(vgrads, ((0, 0), (0, own - vrows), (0, 0))).reshape(width, 128)
    g_qkv = scatter_sum(
        jnp.concatenate(
            [t_dot(x_own, dq), t_dot(x_all, jnp.concatenate([dk, dv], axis=1)), vgrads], axis=1
        )
    )
    dx = dot_t(jnp.concatenate([dk, dv], axis=1), wkv).reshape(seqs, ctx_n, rows, width)
    dx_own = dot_t(dq, wq) + jnp.where(t == 0, grad_one, 0.0)
    dx = jnp.concatenate(
        [dx[:, :1] + dx_own.reshape(seqs, 1, rows, width), dx[:, 1:]], axis=1
    ).astype(BF)
    back = perm.T
    keep = jnp.where(t == 0, back[:, :half], back[:, half:])
    give = jnp.where(t == 0, back[:, half:], back[:, :half])
    flat = dx.reshape(seqs * cap, width)
    kept = dot(flat, keep) + tp_swap(dot(flat, give).astype(BF)).astype(F32)
    kept = kept.astype(BF).reshape(seqs, ctx_n, rows, half)
    mine = sum(from_ctx(kept[:, k], k).astype(F32) for k in range(ctx_n)).astype(BF)
    other = tp_swap(mine)
    in_grad = jnp.concatenate(
        [jnp.where(t == 0, mine, other), jnp.where(t == 0, other, mine)], axis=-1
    )
    live3 = own_live[:, :, None]
    input_grad = jnp.where(live3, in_grad, jnp.zeros((), BF))
    outputs = jnp.where(
        live3, dot(out_rel, back).astype(BF).reshape(seqs, rows, width), jnp.zeros((), BF)
    )
    gv = g_qkv[:vrows, 3 * hcols :].reshape(-1)

    def own_vec(i):
        return gv[at[i] : at[i] + cuts[i]]

    return (
        outputs,
        input_grad,
        g_qkv[:, :hcols],
        g_qkv[:, hcols : 2 * hcols],
        g_qkv[:, 2 * hcols : 3 * hcols],
        own_vec(0)[None],
        own_vec(1)[None],
        g_out.T,
        own_vec(2),
        own_vec(3),
        own_vec(4),
        g_up,
        own_vec(5)[None],
        g_down.T,
        own_vec(6),
        own_vec(7),
        own_vec(8),
    )


def solution(mesh):
    both = ("fsdp", "ctx")
    rows = P("fsdp", "ctx", None)
    col = P(both, "tp")
    row = P("tp", both)
    vec = P(both)
    params = (col, col, col, row, row, row, vec, vec, vec, col, row, row, vec, vec, vec)

    def body(*args):
        own = args[12].shape[0]
        whole_tiles = own % 16 == 0 and mesh.shape["ctx"] == 4
        return (fast_body if whole_tiles else general_body)(*args)

    return jax.shard_map(
        body,
        mesh=mesh,
        in_specs=(rows, rows, P(), P(), P()) + params,
        out_specs=(rows, rows) + params,
        check_vma=False,
    )
```
